32 devices in a mesh: seq: 8 (over z, y), head: 2 (over x), slide: 2 (over core).
Axes of the slice: x: 2, y: 2, z: 4, core: 2. Of those that a mesh axis runs over, the one named last changes fastest.
Arguments:
- query_rows: bfloat16 [8192, 1536], P(('slide', 'seq'), 'head'), parts along dimension 0, may hold values from -32 to 32
- key_rows: bfloat16 [8192, 1536], P(('slide', 'seq'), 'head'), parts along dimension 0, may hold values from -32 to 32
- value_rows: bfloat16 [8192, 1536], P(('slide', 'seq'), 'head'), parts along dimension 0, may hold values from -6 to 6
- patch_valid: int32 [8192], P(('slide', 'seq')), parts along dimension 0, may hold values 0 or 1
- segment_lengths: int32 [4, 3], replicated, may hold values from 256 to 2048, as said below
- dilation: int32 [4, 3], replicated, may hold values from 1 to 8, as said below
- step_sizes: float32 [24, 8192], P('head', ('slide', 'seq')), parts along dimension 1, may hold values from 0.02 to 0.2
- decay_rates: float32 [24, 8192], P('head', ('slide', 'seq')), parts along dimension 1, may hold values from 0 to 2
- state_in: bfloat16 [8192, 128], P(('slide', 'seq')), parts along dimension 0, may hold values from -6 to 6
- state_out: bfloat16 [8192, 128], P(('slide', 'seq')), parts along dimension 0, may hold values from -0.5 to 0.5
- gate_in: bfloat16 [8192, 1536], P(('slide', 'seq'), 'head'), parts along dimension 0, may hold values from -6 to 6
- skip_weight: float32 [24], P('head'), may hold values from 0.5 to 2
- norm_gain: float32 [1536], P('head'), may hold values from 0.1 to 1.9
Outputs:
- attended: bfloat16 [8192, 1536], P(('slide', 'seq'), 'head'), parts along dimension 0
- scanned: bfloat16 [8192, 1536], P(('slide', 'seq'), 'head'), parts along dimension 0
The draws below stay inside these ranges and needn't reach their ends.
There are 2 independent parts, one for each index of `slide`. The reference program is written for one: setup_inputs(seed, part) draws one part's arguments, and reference() takes and returns one part's arrays. A program takes and returns all parts, laid end to end along the dimension named above; an argument that names none is the same for every part. Nothing has to cross between parts.
Inputs may be any that keep to these rules, and one draw needn't show every extreme that they name: `segment_lengths`: every segment length divides 4 * 512 and is a multiple of the dilation of the same group and configuration; in every group the first configuration's segment length divides 512 and the last configuration's segment length is 2048. `dilation`: powers of two; the first configuration's dilation is 1 in every group, every other configuration's dilation is 2 or more.
All inputs are finite; a program needn't handle non-finite values. No bound on the sum of `patch_valid` on one device may be relied on, other than what follows from the above.
Results may differ from the reference program's by a relative error of at most 0.0075.
Values may be sent and summed in bfloat16 or wider, within the bound.
A program may use at most 128 MiB of HBM per device.

```python
import math
import jax
import jax.numpy as jnp
from jax import lax

HEADS = 24
HEAD_DIM = 64
STATE = 128
GROUPS = 4
CONFIGS = 3
SPAN_DEV = 4
TOK_DEV = 512
SLIDE_TOKEN_LEN = 4096


def drawn_rows(key, role_index):
    full_shape = (SLIDE_TOKEN_LEN, HEADS, HEAD_DIM)
    own_key = jax.random.fold_in(key, 11 + role_index)
    result = jnp.clip(jax.random.normal(own_key, full_shape, jnp.float32), -6.0, 6.0)
    return result.reshape(SLIDE_TOKEN_LEN, HEADS * HEAD_DIM)


def draw_query_rows(key, part):
    return drawn_rows(key, 0).astype(jnp.bfloat16)


def draw_key_rows(key, part):
    return drawn_rows(key, 1).astype(jnp.bfloat16)


def plan_table(key):
    chosen_group = jax.random.randint(jax.random.fold_in(key, 100), (), 0, GROUPS)
    picks = jax.random.randint(jax.random.fold_in(key, 101), (GROUPS, 4), 0, 2)
    middle_pick = jax.random.randint(jax.random.fold_in(key, 102), (GROUPS,), 0, 4)
    first_group = (jnp.arange(GROUPS, dtype=jnp.int32) == chosen_group).astype(jnp.int32)
    nearest = TOK_DEV // 2 * (1 + picks[:, 0] * (1 - first_group))
    middle_table = jnp.array([TOK_DEV // 2, TOK_DEV, 2 * TOK_DEV, SPAN_DEV * TOK_DEV], jnp.int32)
    middle = middle_table[middle_pick]
    widest = jnp.full((GROUPS,), SPAN_DEV * TOK_DEV, jnp.int32)
    stride_mid = 2 * (1 + picks[:, 2])
    stride_far = 4 * (1 + jnp.maximum(picks[:, 3], first_group))
    lengths = jnp.stack([nearest, middle, widest], axis=1).astype(jnp.int32)
    strides = jnp.stack([jnp.ones((GROUPS,), jnp.int32), stride_mid, stride_far], axis=1).astype(jnp.int32)
    return (lengths, strides)


def draw_segment_lengths(key, part):
    return plan_table(key)[0]


def draw_dilation(key, part):
    return plan_table(key)[1]


def draw_decay_rates(key, part):
    full_shape = (HEADS, SLIDE_TOKEN_LEN)
    fast_share = 0.4
    picks = jax.random.uniform(jax.random.fold_in(key, 1), (HEADS, 1), jnp.float32)
    rapid_decay = picks < fast_share
    brisk_branch = jnp.exp(jax.random.uniform(jax.random.fold_in(key, 2), full_shape, jnp.float32, math.log(1.0 / 60.0), math.log(1.0 / 25.0)))
    gentle_decay = jnp.exp(jax.random.uniform(jax.random.fold_in(key, 3), full_shape, jnp.float32, math.log(0.1), math.log(0.5))) / SLIDE_TOKEN_LEN
    spike_location = jax.random.randint(jax.random.fold_in(key, 4), (3,), 0, SLIDE_TOKEN_LEN)
    spike_length = jnp.exp(jax.random.uniform(jax.random.fold_in(key, 5), (3,), jnp.float32, math.log(0.22), math.log(0.5)))
    token_places = jnp.arange(SLIDE_TOKEN_LEN, dtype=jnp.int32)
    spike_groups = jnp.sum(jnp.where(token_places[None, :] == spike_location[:, None], spike_length[:, None], 0.0), axis=0)
    return jnp.where(rapid_decay, brisk_branch, gentle_decay) + spike_groups[None, :]


def with_ends(values, key, least, high):
    spot = [jax.random.randint(jax.random.fold_in(key, axis), (), 0, length) for axis, length in enumerate(values.shape)]
    longest = values.shape.index(max(values.shape))
    neighbour = spot[:longest] + [(spot[longest] + 1) % values.shape[longest]] + spot[longest + 1:]
    return values.at[tuple(spot)].set(least).at[tuple(neighbour)].set(high)


def steps_of(stream_key, extent, split, low, largest):
    def one(dim, blocks):
        heights = jax.random.uniform(jax.random.fold_in(jax.random.fold_in(stream_key, 6), dim), (blocks,), jnp.float32, low / len(split), largest / len(split))
        return jnp.repeat(jnp.exp(heights), extent[dim] // blocks).reshape((-1,) + (1,) * (len(extent) - dim - 1))

    level = one(*split[0])
    for cut in split[1:]:
        level = level * one(*cut)
    return level


def gaussian(key, shape, spread, limit, split=(), held_as=jnp.bfloat16):
    loudness = steps_of(key, shape, split, -0.22, 0.18) if split else 1.0
    drawn = jax.random.normal(key, shape, jnp.float32) * spread * loudness
    return jnp.minimum(jnp.maximum(drawn, -limit), limit).astype(held_as)


def setup_inputs(seed: int = 0, part: int = 0) -> dict:
    key_list = jax.random.split(jax.random.key(seed), 14)
    own_keys = jax.random.split(jax.random.fold_in(key_list[13], part), 14)
    return {
        "query_rows": draw_query_rows(jax.random.fold_in(jax.random.fold_in(key_list[13], part), 71), part),
        "key_rows": draw_key_rows(jax.random.fold_in(jax.random.fold_in(key_list[13], part), 71), part),
        "value_rows": gaussian(own_keys[2], (SLIDE_TOKEN_LEN, HEADS * HEAD_DIM), 1.0, 6.0, ((0, 8), (1, 2))),
        "patch_valid": with_ends((jax.random.randint(own_keys[3], (SLIDE_TOKEN_LEN,), 0, 8) < 7).astype(jnp.int32), jax.random.fold_in(own_keys[3], 1), 0, 1),
        "segment_lengths": draw_segment_lengths(jax.random.fold_in(key_list[13], 71), part),
        "dilation": draw_dilation(jax.random.fold_in(key_list[13], 71), part),
        "step_sizes": jnp.clip(jnp.exp(math.log(0.2) - 2.3025851 * jax.random.uniform(own_keys[6], (HEADS, SLIDE_TOKEN_LEN), jnp.float32) ** steps_of(own_keys[6], (HEADS, SLIDE_TOKEN_LEN), ((0, 2), (1, 8)), -0.2, 0.2)), 0.02, 0.2),
        "decay_rates": draw_decay_rates(jax.random.fold_in(jax.random.fold_in(key_list[13], part), 71), part),
        "state_in": gaussian(own_keys[8], (SLIDE_TOKEN_LEN, STATE), 1.0, 6.0, ((0, 8),)),
        "state_out": gaussian(own_keys[9], (SLIDE_TOKEN_LEN, STATE), STATE ** -0.5, 0.5, ((0, 8),)),
        "gate_in": gaussian(own_keys[10], (SLIDE_TOKEN_LEN, HEADS * HEAD_DIM), 1.0, 6.0, ((0, 8), (1, 2))),
        "skip_weight": jnp.clip(jnp.exp(math.log(2.0) - 1.3862944 * jax.random.uniform(key_list[11], (HEADS,), jnp.float32) ** steps_of(key_list[11], (HEADS,), ((0, 2),), -0.2, 0.2)), 0.5, 2.0),
        "norm_gain": jnp.clip(1.0 + 0.18 * jax.random.normal(key_list[12], (HEADS * HEAD_DIM,), jnp.float32), 0.1, 1.9),
    }


def admitted_count(query_pos, key_pos, key_valid, head_ids, widths, strides):
    offsets = head_ids[:, None] % strides
    counted = jnp.zeros((head_ids.shape[0], query_pos.shape[0], key_pos.shape[0]), jnp.float32)
    for config in range(CONFIGS):
        seg_width = widths[:, config][:, None]
        stride_now = strides[:, config][:, None]
        offset_now = offsets[:, config][:, None]
        query_seg = query_pos[None, :] // seg_width
        key_seg = key_pos[None, :] // seg_width
        query_on = query_pos[None, :] % stride_now == offset_now
        key_on = key_pos[None, :] % stride_now == offset_now
        joined = (query_seg[:, :, None] == key_seg[:, None, :]) & query_on[:, :, None] & key_on[:, None, :]
        counted = counted + joined.astype(jnp.float32)
    opened = (key_valid[None, :] > 0) | (query_pos[:, None] == key_pos[None, :])
    return counted * opened[None].astype(jnp.float32)

def reference(query_rows, key_rows, value_rows, patch_valid, segment_lengths, dilation, step_sizes, decay_rates, state_in, state_out, gate_in, skip_weight, norm_gain):
    score_scale = HEAD_DIM ** (-0.5)
    head_ids = jnp.arange(HEADS, dtype=jnp.int32)
    group_ids = head_ids // (HEADS // GROUPS)
    widths = segment_lengths[group_ids]
    strides = dilation[group_ids]
    window = SPAN_DEV * TOK_DEV

    def one_block(block_idx):
        row_start = (block_idx * TOK_DEV).astype(jnp.int32)
        key_start = (block_idx // SPAN_DEV * window).astype(jnp.int32)
        query_blk = lax.dynamic_slice_in_dim(query_rows, row_start, TOK_DEV, 0).reshape(TOK_DEV, HEADS, HEAD_DIM).astype(jnp.float32)
        key_blk = lax.dynamic_slice_in_dim(key_rows, key_start, window, 0).reshape(window, HEADS, HEAD_DIM).astype(jnp.float32)
        value_blk = lax.dynamic_slice_in_dim(value_rows, key_start, window, 0).reshape(window, HEADS, HEAD_DIM).astype(jnp.float32)
        valid_keys = lax.dynamic_slice_in_dim(patch_valid, key_start, window, 0)
        valid_here = lax.dynamic_slice_in_dim(patch_valid, row_start, TOK_DEV, 0).astype(jnp.float32)
        query_pos = row_start + jnp.arange(TOK_DEV, dtype=jnp.int32)
        key_pos = key_start + jnp.arange(window, dtype=jnp.int32)
        scores = jnp.einsum('thd,shd->hts', query_blk, key_blk) * score_scale
        counted = admitted_count(query_pos, key_pos, valid_keys, head_ids, widths, strides)
        admits = counted > 0
        row_top = lax.optimization_barrier(jnp.max(jnp.where(admits, scores, -jnp.inf), axis=-1, keepdims=True))
        weights = counted * jnp.exp(jnp.where(admits, scores, row_top) - row_top)
        row_total = lax.optimization_barrier(jnp.sum(weights, axis=-1))
        rounded = lax.optimization_barrier(weights.astype(jnp.bfloat16)).astype(jnp.float32)
        mixing = jnp.einsum('hts,shd->thd', rounded, value_blk)
        result = mixing / row_total.T[:, :, None] * valid_here[:, None, None]
        return result.reshape(TOK_DEV, HEADS * HEAD_DIM).astype(jnp.bfloat16)
    block_count = SLIDE_TOKEN_LEN // TOK_DEV
    attended = lax.map(one_block, jnp.arange(block_count, dtype=jnp.int32)).reshape(SLIDE_TOKEN_LEN, HEADS * HEAD_DIM)
    highest = lax.Precision.HIGHEST
    inputs_all = value_rows.reshape(block_count, TOK_DEV, HEADS, HEAD_DIM).astype(jnp.float32)
    steps_blk = step_sizes.reshape(HEADS, block_count, TOK_DEV).transpose(1, 0, 2)
    rates_blk = decay_rates.reshape(HEADS, block_count, TOK_DEV).transpose(1, 0, 2)
    valid_blk = patch_valid.reshape(block_count, TOK_DEV).astype(jnp.float32)
    into_blk = state_in.reshape(block_count, TOK_DEV, STATE).astype(jnp.float32)
    read_blk = state_out.reshape(block_count, TOK_DEV, STATE).astype(jnp.float32)
    gate_blk = gate_in.reshape(block_count, TOK_DEV, HEADS, HEAD_DIM).astype(jnp.float32)
    token_places = jnp.arange(TOK_DEV, dtype=jnp.int32)
    causal = token_places[:, None] >= token_places[None, :]

    def advance(carried, pieces):
        inputs_now, steps_now, rates_now, valid_now, into_now, read_now, gate_now = pieces
        log_decay = -jnp.cumsum(rates_now, axis=1)
        driven = inputs_now * (steps_now.T * valid_now[:, None])[:, :, None]
        coupling = jnp.dot(read_now, into_now.T, precision=highest)
        decays = jnp.exp(jnp.where(causal[None], log_decay[:, :, None] - log_decay[:, None, :], -jnp.inf))
        within = jnp.einsum('hts,shp->thp', decays * coupling[None], driven, precision=highest)
        from_before = jnp.exp(log_decay).T[:, :, None] * jnp.einsum('tn,hpn->thp', read_now, carried, precision=highest)
        readout = within + from_before + skip_weight[None, :, None] * inputs_now
        gated_out = readout * jax.nn.silu(gate_now)
        normed = gated_out * lax.rsqrt(lax.optimization_barrier(jnp.mean(gated_out * gated_out, axis=-1, keepdims=True)) + 1e-05) * norm_gain.reshape(HEADS, HEAD_DIM)
        to_end = jnp.exp(log_decay[:, -1:] - log_decay)
        end_state = jnp.einsum('shp,sn->hpn', driven * to_end.T[:, :, None], into_now, precision=highest)
        carried = jnp.exp(log_decay[:, -1])[:, None, None] * carried + end_state
        return (carried, normed.reshape(TOK_DEV, HEADS * HEAD_DIM).astype(jnp.bfloat16))
    initial = jnp.zeros((HEADS, HEAD_DIM, STATE), jnp.float32)
    final_state, scanned = lax.scan(advance, initial, (inputs_all, steps_blk, rates_blk, valid_blk, into_blk, read_blk, gate_blk))
    scanned = scanned.reshape(SLIDE_TOKEN_LEN, HEADS * HEAD_DIM)
    return (attended, scanned)
```

```python
import functools

import jax
import jax.numpy as jnp
from jax import lax
from jax.experimental import pallas as pl
from jax.experimental.pallas import tpu as pltpu
from jax.sharding import PartitionSpec as P

HEADS = 24
HEAD_DIM = 64
GROUPS = 4
SPAN_DEV = 4
PAIR = 2 * HEAD_DIM
F32 = jnp.float32
BF16 = jnp.bfloat16
HIGHEST = lax.Precision.HIGHEST
MESH = pl.DeviceIdType.MESH
NEG = -jnp.inf


def nt(a, b, precision=None):
    return lax.dot_general(
        a, b, (((1,), (1,)), ((), ())), preferred_element_type=F32, precision=precision
    )


def nn(a, b, precision=None):
    return lax.dot_general(
        a, b, (((1,), (0,)), ((), ())), preferred_element_type=F32, precision=precision
    )


def iota(shape, axis):
    return lax.broadcasted_iota(jnp.int32, shape, axis)


def three_parts(row):
    high = row.astype(BF16).astype(F32)
    mid = (row - high).astype(BF16).astype(F32)
    return high, mid, row - high - mid


def kernel(
    ranks,
    covers,
    seg_ref,
    dil_ref,
    skip_ref,
    q_ref,
    k_ref,
    v_ref,
    valid_ref,
    steps_ref,
    rates_ref,
    into_ref,
    read_ref,
    gate_ref,
    gain_ref,
    att_ref,
    scan_ref,
    perm,
    unperm,
    q_same,
    q_other,
    k_other,
    v_other,
    sent,
    got,
    opened,
    valid_rows,
    valid_cols,
    acc_same,
    out_other,
    top_same,
    total_same,
    log_row,
    log_col,
    drive_row,
    into_t,
    coupling,
    within,
    s_sent,
    s_got,
    kv_send,
    kv_recv,
    st_send,
    st_recv,
):
    rows, width = q_ref.shape
    half = rows // 2
    pairs = width // PAIR
    head_count = 2 * pairs
    group_heads = HEADS // GROUPS
    rank = lax.axis_index("seq")
    first_head = lax.axis_index("head") * head_count
    base = rank * rows
    v_base = pairs * half
    valid_base = 2 * pairs * half
    shifts = sorted({1, 2, *covers})

    barrier = pltpu.get_barrier_semaphore()
    for mask in range(1, SPAN_DEV):
        pl.semaphore_signal(barrier, inc=1, device_id={"seq": rank ^ mask}, device_id_type=MESH)
    for shift in shifts:
        for other in (rank + shift, rank + ranks - shift):
            pl.semaphore_signal(
                barrier,
                inc=1,
                device_id={"seq": lax.rem(other, ranks)},
                device_id_type=MESH,
            )

    low_lane = iota((half, PAIR), 1) < HEAD_DIM
    r_id = iota((rows, rows), 0)
    c_id = iota((rows, rows), 1)
    perm[...] = jnp.where(c_id == 2 * (r_id % half) + r_id // half, 1.0, 0.0).astype(BF16)
    unperm[...] = jnp.where(r_id == 2 * (c_id % half) + c_id // half, 1.0, 0.0).astype(BF16)
    valid_f = valid_ref[...].astype(F32)
    sorted_valid = nt(jnp.broadcast_to(valid_f, (8, rows)).astype(BF16), perm[...])[0:1]
    valid_rows[0:1] = sorted_valid[:, :half]
    valid_rows[1:2] = sorted_valid[:, half:]
    line = iota((16, 128), 0)
    lines = jnp.zeros((16, 128), F32)
    for piece in range(rows // 128):
        lines = jnp.where(line == piece, sorted_valid[:, piece * 128 : (piece + 1) * 128], lines)
    sent[pl.ds(valid_base, 16)] = lines.astype(BF16)

    def lanes_of(pair):
        return pl.ds(pl.multiple_of(pair * PAIR, PAIR), PAIR)

    def rows_of(pair, start):
        return pl.ds(pl.multiple_of(start + pair * half, half), half)

    for pair in range(pairs):
        cols = slice(pair * PAIR, (pair + 1) * PAIR)
        k_sorted = nn(perm[...], k_ref[:, cols])
        v_sorted = nn(perm[...], v_ref[:, cols])
        k_even, k_odd = k_sorted[:half], k_sorted[half:]
        v_even, v_odd = v_sorted[:half], v_sorted[half:]
        sent[pair * half : (pair + 1) * half] = jnp.where(low_lane, k_even, k_odd).astype(BF16)
        sent[v_base + pair * half : v_base + (pair + 1) * half] = jnp.where(
            low_lane, v_even, v_odd
        ).astype(BF16)
        k_other[pair] = jnp.where(low_lane, k_odd, k_even).astype(BF16)
        v_other[pair] = jnp.where(low_lane, v_odd, v_even).astype(BF16)

    pl.semaphore_wait(barrier, SPAN_DEV - 1 + 2 * len(shifts))

    kv_copies = []
    for mask in range(1, SPAN_DEV):
        kv_copies.append(
            pltpu.make_async_remote_copy(
                src_ref=sent,
                dst_ref=got.at[mask - 1],
                send_sem=kv_send.at[mask - 1],
                recv_sem=kv_recv.at[mask - 1],
                device_id={"seq": rank ^ mask},
                device_id_type=MESH,
            )
        )

    rates = rates_ref[...]
    upper = jnp.where(r_id <= c_id, 1.0, 0.0)
    lower = jnp.where(r_id >= c_id, 1.0, 0.0)
    log_all = -nn(rates, upper, HIGHEST)
    columns = -nt(lower, rates, HIGHEST)
    for head in range(head_count):
        log_col[head] = jnp.broadcast_to(columns[:, head : head + 1], (rows, 128))
    drive_all = steps_ref[...] * valid_f
    for head in range(head_count):
        log_row[head] = log_all[head : head + 1]
        drive_row[head] = drive_all[head : head + 1]
    into_t[...] = into_ref[...].astype(F32).T
    log_end = log_all[:, rows - 1 : rows]
    own_lane = iota((head_count, width), 1) // HEAD_DIM == iota((head_count, width), 0)
    own_log = jnp.sum(jnp.where(own_lane, log_end, 0.0), axis=0, keepdims=True)
    to_end = drive_all * jnp.exp(log_end - log_all)
    state_dim = into_ref.shape[1]
    low_state = iota((state_dim, PAIR), 1) < HEAD_DIM
    for pair in range(pairs):
        cols = slice(pair * PAIR, (pair + 1) * PAIR)
        parts = []
        for odd in range(2):
            head = 2 * pair + odd
            scaled = (into_t[...] * to_end[head : head + 1]).astype(BF16)
            parts.append(nn(scaled, v_ref[:, cols]))
        s_sent[0, 0:state_dim, cols] = jnp.where(low_state, parts[0], parts[1]).astype(BF16)
    tail = iota((16, width), 0)

    def tail_rows(log_sum):
        high, mid, low = three_parts(log_sum)
        return jnp.where(
            tail == 0, high, jnp.where(tail == 1, mid, jnp.where(tail == 2, low, 0.0))
        ).astype(BF16)

    s_sent[0, state_dim : state_dim + 16] = tail_rows(own_log)

    def state_copy(source, slot, shift):
        return pltpu.make_async_remote_copy(
            src_ref=s_sent.at[source],
            dst_ref=s_got.at[slot],
            send_sem=st_send.at[slot],
            recv_sem=st_recv.at[slot],
            device_id={"seq": lax.rem(rank + shift, ranks)},
            device_id_type=MESH,
        )

    def start(copy, shift):
        @pl.when(rank + shift < ranks)
        def _():
            copy.start()

    def arrived(copy, shift):
        @pl.when(rank >= shift)
        def _():
            copy.wait_recv()

    def left(copy, shift):
        @pl.when(rank + shift < ranks)
        def _():
            copy.wait_send()

    def summary(slot, shift):
        there = rank >= shift
        state = jnp.where(there, s_got[slot, 0:state_dim].astype(F32), 0.0)
        end = s_got[slot, state_dim : state_dim + 16].astype(F32)
        log_sum = jnp.where(there, end[0:1] + end[1:2] + end[2:3], 0.0)
        return log_sum, state

    def joined(earlier, later):
        return earlier[0] + later[0], jnp.exp(later[0]) * earlier[1] + later[1]

    near = state_copy(0, 0, 1)
    next_near = state_copy(0, 1, 2)
    start(near, 1)
    start(next_near, 2)
    for copy in kv_copies:
        copy.start()

    for pair in range(pairs):
        cols = slice(pair * PAIR, (pair + 1) * PAIR)
        q_sorted = nn(perm[...], q_ref[:, cols]) * HEAD_DIM ** (-0.5)
        q_even, q_odd = q_sorted[:half], q_sorted[half:]
        q_same[pair] = jnp.where(low_lane, q_even, q_odd).astype(BF16)
        q_other[pair] = jnp.where(low_lane, q_odd, q_even).astype(BF16)
    eye = iota((half, half), 0) == iota((half, half), 1)
    for odd in range(2):
        opened[odd] = jnp.where(eye, 1.0, jnp.broadcast_to(valid_rows[odd : odd + 1], (half, half)))
    valid_cols[...] = nt(perm[...], jnp.broadcast_to(valid_f, (PAIR, rows)).astype(BF16))
    coupling[...] = jnp.where(r_id >= c_id, nt(read_ref[...], into_ref[...]), 0.0)

    def twice(column):
        return jnp.concatenate([column] * (half // 128), axis=1)

    q_line = 2 * iota((half, 128), 0)
    k_line = 2 * iota((1, half), 1)

    def plan(pair, odd):
        head = first_head + 2 * pair + odd
        group = head // group_heads
        spans = [seg_ref[group, config] for config in range(3)]
        strides = [dil_ref[group, config] for config in range(3)]
        return head, spans, strides

    def code(place, head, span, stride, missing):
        on = (place & (stride - 1)) == (head & (stride - 1))
        return jnp.where(on, place & -span, missing)

    def one(flag):
        return jnp.where(flag, 1.0, 0.0)

    def own_head(odd):
        return low_lane if odd == 0 else jnp.logical_not(low_lane)

    def local_pair(pair, _):
        same_pieces, other_pieces = [], []
        k_s = sent[rows_of(pair, 0), :]
        v_s = sent[rows_of(pair, v_base), :]
        k_o, v_o = k_other[pair], v_other[pair]
        for odd in range(2):
            head, spans, strides = plan(pair, odd)
            mine = own_head(odd)
            zero = jnp.zeros((half, PAIR), BF16)
            q_s = jnp.where(mine, q_same[pair], zero)
            q_o = jnp.where(mine, q_other[pair], zero)
            at_s = base + q_line + odd
            at_o = base + q_line + (1 - odd)
            key_s = base + k_line + odd
            key_o = base + k_line + (1 - odd)
            open_s = valid_rows[odd : odd + 1] > 0
            open_o = valid_rows[1 - odd : 2 - odd] > 0
            near_s = twice(at_s & -spans[0])
            near_o = twice(at_o & -spans[0])
            kn_s = key_s & -spans[0]
            kn_o = key_o & -spans[0]
            count = one(near_s == kn_s)
            for config in (1, 2):
                count = count + one(
                    twice(code(at_s, head, spans[config], strides[config], -1))
                    == code(key_s, head, spans[config], strides[config], -2)
                )
            count = count * opened[odd]
            a = jnp.where(count > 0, nt(q_s, k_s), NEG)
            b = jnp.where(near_s == jnp.where(open_o, kn_o, -2), nt(q_s, k_o), NEG)
            top = jnp.maximum(
                jnp.max(a, axis=1, keepdims=True), jnp.max(b, axis=1, keepdims=True)
            )
            wa = count * jnp.exp(a - top)
            wb = jnp.exp(b - top)
            total = jnp.sum(wa, axis=1, keepdims=True) + jnp.sum(wb, axis=1, keepdims=True)
            top_same[2 * pair + odd] = jnp.broadcast_to(top, (half, 128))
            total_same[2 * pair + odd] = jnp.broadcast_to(total, (half, 128))
            same_pieces.append(nn(wa.astype(BF16), v_s) + nn(wb.astype(BF16), v_o))
            a = jnp.where(near_o == jnp.where(open_s, kn_s, -2), nt(q_o, k_s), NEG)
            b = jnp.where(one(near_o == kn_o) * opened[1 - odd] > 0, nt(q_o, k_o), NEG)
            top = jnp.maximum(
                jnp.max(a, axis=1, keepdims=True), jnp.max(b, axis=1, keepdims=True)
            )
            wa = jnp.exp(a - top)
            wb = jnp.exp(b - top)
            total = jnp.sum(wa, axis=1, keepdims=True) + jnp.sum(wb, axis=1, keepdims=True)
            other_pieces.append((nn(wa.astype(BF16), v_s) + nn(wb.astype(BF16), v_o)) / total)
        acc_same[pair] = jnp.where(low_lane, same_pieces[0], same_pieces[1])
        out_other[pair] = jnp.where(low_lane, other_pieces[0], other_pieces[1])
        return 0

    def within_pair(pair, _):
        block = 128
        low_block = iota((block, PAIR), 1) < HEAD_DIM
        for step in range(rows // block):
            here = slice(step * block, (step + 1) * block)
            parts = []
            for odd in range(2):
                head = 2 * pair + odd
                at = log_col[head, here]
                tiles = []
                for back in range(step + 1):
                    there = slice(back * block, (back + 1) * block)
                    decay = jnp.exp(jnp.minimum(at - log_row[head, :, there], 0.0))
                    tiles.append(
                        (decay * coupling[here, there] * drive_row[head, :, there]).astype(BF16)
                    )
                mix = jnp.concatenate(tiles, axis=1) if step else tiles[0]
                parts.append(nn(mix, v_ref[0 : (step + 1) * block, lanes_of(pair)]))
            within[pair, here] = jnp.where(low_block, parts[0], parts[1])
        return 0

    lax.fori_loop(0, pairs // 2, within_pair, 0)
    arrived(near, 1)
    arrived(next_near, 2)
    before = joined(summary(1, 2), summary(0, 1))
    chain = []
    for index, shift in enumerate(covers):
        s_sent[index + 1, 0:state_dim] = before[1].astype(BF16)
        s_sent[index + 1, state_dim : state_dim + 16] = tail_rows(before[0])
        copy = state_copy(index + 1, index + 2, shift)
        start(copy, shift)
        chain.append(copy)
        if index == 0:
            lax.fori_loop(pairs // 2, pairs, within_pair, 0)
        if index == 1:
            lax.fori_loop(0, pairs, local_pair, 0)
        arrived(copy, shift)
        before = joined(summary(index + 2, shift), before)
    into_t_before = before[1].astype(BF16)
    spread = s_sent.at[0]
    left(near, 1)
    left(next_near, 2)
    for copy, shift in zip(chain, covers):
        left(copy, shift)
    spread[0:state_dim] = into_t_before

    low_rows = iota((rows, PAIR), 1) < HEAD_DIM
    same_head = jnp.where(
        iota((PAIR, PAIR), 0) // HEAD_DIM == iota((PAIR, PAIR), 1) // HEAD_DIM, 1.0, 0.0
    ).astype(BF16)

    def finish_scan(pair, _):
        cols = lanes_of(pair)
        value = v_ref[:, cols].astype(F32)
        since = jnp.exp(jnp.where(low_rows, log_col[2 * pair], log_col[2 * pair + 1]))
        carried = since * nn(read_ref[...], spread[0:state_dim, cols])
        skip = jnp.where(low_rows[0:1], skip_ref[2 * pair], skip_ref[2 * pair + 1])
        readout = within[pair] + carried + skip * value
        gate = gate_ref[:, cols].astype(F32)
        gated = readout * (gate / (1.0 + jnp.exp(-gate)))
        square = gated * gated
        high = square.astype(BF16)
        low = (square - high.astype(F32)).astype(BF16)
        mean = (nn(high, same_head) + nn(low, same_head)) * (1.0 / HEAD_DIM)
        scan_ref[:, cols] = (gated * lax.rsqrt(mean + 1e-05) * gain_ref[:, cols]).astype(BF16)
        return 0

    lax.fori_loop(0, pairs, finish_scan, 0)

    def far_pair(mask, last, valid_s, pair):
        pieces = []
        slot = mask - 1
        far_base = (rank ^ mask) * rows
        k_s = got[slot, rows_of(pair, 0), :]
        v_s = got[slot, rows_of(pair, v_base), :]
        scales, totals = [], []
        for odd in range(2):
            head, spans, strides = plan(pair, odd)
            q_s = jnp.where(own_head(odd), q_same[pair], jnp.zeros((half, PAIR), BF16))
            at_s = base + q_line + odd
            key_s = far_base + k_line + odd
            count = None
            for config in (1, 2):
                key_code = code(key_s, head, spans[config], strides[config], -2)
                key_code = jnp.where(valid_s[odd] > 0, key_code, -2)
                hit = one(
                    twice(code(at_s, head, spans[config], strides[config], -1)) == key_code
                )
                count = hit if count is None else count + hit
            a = jnp.where(count > 0, nt(q_s, k_s), NEG)
            old_top = top_same[2 * pair + odd]
            top = jnp.maximum(old_top, jnp.max(a, axis=1, keepdims=True))
            w = count * jnp.exp(a - twice(top))
            scale = jnp.exp(old_top - top)
            total = total_same[2 * pair + odd] * scale + jnp.sum(w, axis=1, keepdims=True)
            if not last:
                top_same[2 * pair + odd] = top
                total_same[2 * pair + odd] = total
            pieces.append(nn(w.astype(BF16), v_s))
            scales.append(scale)
            totals.append(total)
        acc = acc_same[pair] * jnp.where(low_lane, scales[0], scales[1]) + jnp.where(
            low_lane, pieces[0], pieces[1]
        )
        if not last:
            acc_same[pair] = acc
            return
        same = acc / jnp.where(low_lane, totals[0], totals[1])
        other = out_other[pair]
        even = jnp.where(low_lane, same, other) * valid_cols[0:half]
        odd_rows = jnp.where(low_lane, other, same) * valid_cols[half:]
        both = jnp.concatenate([even, odd_rows], axis=0).astype(BF16)
        att_ref[:, lanes_of(pair)] = nn(unperm[...], both).astype(BF16)

    for mask in range(1, SPAN_DEV):
        kv_copies[mask - 1].wait_recv()
        far_valid = got[mask - 1, pl.ds(valid_base, 16)].astype(F32)
        per = half // 128
        valid_s = [
            jnp.concatenate(
                [far_valid[odd * per + i : odd * per + i + 1] for i in range(per)], axis=1
            )
            for odd in range(2)
        ]

        def far(pair, _, mask=mask, valid_s=valid_s):
            far_pair(mask, mask == SPAN_DEV - 1, valid_s, pair)
            return 0

        lax.fori_loop(0, pairs, far, 0)
    for copy in kv_copies:
        copy.wait_send()


def per_device(
    ranks,
    query_rows,
    key_rows,
    value_rows,
    patch_valid,
    segment_lengths,
    dilation,
    step_sizes,
    decay_rates,
    state_in,
    state_out,
    gate_in,
    skip_weight,
    norm_gain,
):
    rows, width = query_rows.shape
    half = rows // 2
    pairs = width // PAIR
    heads = 2 * pairs
    state = state_in.shape[1]
    covers = []
    cover = 2
    while cover < ranks - 1:
        covers.append(cover)
        cover *= 2
    rounds = len(covers)
    vmem = pl.BlockSpec(memory_space=pltpu.VMEM)
    smem = pl.BlockSpec(memory_space=pltpu.SMEM)
    sent_rows = 2 * pairs * half + 16
    out = jax.ShapeDtypeStruct((rows, width), BF16)
    return pl.pallas_call(
        functools.partial(kernel, ranks, tuple(covers)),
        out_shape=(out, out),
        in_specs=[smem] * 3 + [vmem] * 10,
        out_specs=(vmem, vmem),
        scratch_shapes=[
            pltpu.VMEM((rows, rows), BF16),
            pltpu.VMEM((rows, rows), BF16),
            pltpu.VMEM((pairs, half, PAIR), BF16),
            pltpu.VMEM((pairs, half, PAIR), BF16),
            pltpu.VMEM((pairs, half, PAIR), BF16),
            pltpu.VMEM((pairs, half, PAIR), BF16),
            pltpu.VMEM((sent_rows, PAIR), BF16),
            pltpu.VMEM((SPAN_DEV - 1, sent_rows, PAIR), BF16),
            pltpu.VMEM((2, half, half), F32),
            pltpu.VMEM((8, half), F32),
            pltpu.VMEM((rows, PAIR), F32),
            pltpu.VMEM((pairs, half, PAIR), F32),
            pltpu.VMEM((pairs, half, PAIR), F32),
            pltpu.VMEM((heads, half, 128), F32),
            pltpu.VMEM((heads, half, 128), F32),
            pltpu.VMEM((heads, 1, rows), F32),
            pltpu.VMEM((heads, rows, 128), F32),
            pltpu.VMEM((heads, 1, rows), F32),
            pltpu.VMEM((state, rows), F32),
            pltpu.VMEM((rows, rows), F32),
            pltpu.VMEM((pairs, rows, PAIR), F32),
            pltpu.VMEM((rounds + 1, state + 16, width), BF16),
            pltpu.VMEM((rounds + 2, state + 16, width), BF16),
            pltpu.SemaphoreType.DMA((SPAN_DEV - 1,)),
            pltpu.SemaphoreType.DMA((SPAN_DEV - 1,)),
            pltpu.SemaphoreType.DMA((rounds + 2,)),
            pltpu.SemaphoreType.DMA((rounds + 2,)),
        ],
        compiler_params=pltpu.CompilerParams(
            collective_id=0, has_side_effects=True, vmem_limit_bytes=60000 * 1024
        ),
        name="dilated_ssm",
    )(
        segment_lengths,
        dilation,
        skip_weight,
        query_rows,
        key_rows,
        value_rows,
        patch_valid.reshape(1, rows),
        step_sizes,
        decay_rates,
        state_in,
        state_out,
        gate_in,
        norm_gain.reshape(1, width),
    )


def solution(mesh):
    return jax.shard_map(
        functools.partial(per_device, mesh.shape["seq"]),
        mesh=mesh,
        in_specs=(
            P(("slide", "seq"), "head"),
            P(("slide", "seq"), "head"),
            P(("slide", "seq"), "head"),
            P(("slide", "seq")),
            P(),
            P(),
            P("head", ("slide", "seq")),
            P("head", ("slide", "seq")),
            P(("slide", "seq"), None),
            P(("slide", "seq"), None),
            P(("slide", "seq"), "head"),
            P("head"),
            P("head"),
        ),
        out_specs=(P(("slide", "seq"), "head"), P(("slide", "seq"), "head")),
        check_vma=False,
    )
```

```python
import functools

import jax
import jax.numpy as jnp
from jax import lax
from jax.experimental import pallas as pl
from jax.experimental.pallas import tpu as pltpu
from jax.sharding import PartitionSpec as P

HEADS = 24
HEAD_DIM = 64
GROUPS = 4
SPAN_DEV = 4
PAIR = 2 * HEAD_DIM
F32 = jnp.float32
BF16 = jnp.bfloat16
HIGHEST = lax.Precision.HIGHEST
MESH = pl.DeviceIdType.MESH
NEG = -jnp.inf


def nt(a, b, precision=None):
    return lax.dot_general(
        a, b, (((1,), (1,)), ((), ())), preferred_element_type=F32, precision=precision
    )


def nn(a, b, precision=None):
    return lax.dot_general(
        a, b, (((1,), (0,)), ((), ())), preferred_element_type=F32, precision=precision
    )


def iota(shape, axis):
    return lax.broadcasted_iota(jnp.int32, shape, axis)


def three_parts(row):
    high = row.astype(BF16).astype(F32)
    mid = (row - high).astype(BF16).astype(F32)
    return high, mid, row - high - mid


def kernel(
    ranks,
    seg_ref,
    dil_ref,
    skip_ref,
    q_ref,
    k_ref,
    v_ref,
    valid_ref,
    steps_ref,
    rates_ref,
    into_ref,
    read_ref,
    gate_ref,
    gain_ref,
    att_ref,
    scan_ref,
    perm,
    unperm,
    q_same,
    q_other,
    k_other,
    v_other,
    sent,
    got,
    opened,
    valid_rows,
    valid_cols,
    acc_same,
    out_other,
    top_same,
    total_same,
    log_row,
    log_col,
    drive_row,
    into_t,
    coupling,
    within,
    s_sent,
    s_got,
    before_state,
    kv_send,
    kv_recv,
    st_send,
    st_recv,
):
    rows, width = q_ref.shape
    half = rows // 2
    pairs = width // PAIR
    head_count = 2 * pairs
    group_heads = HEADS // GROUPS
    rank = lax.axis_index("seq")
    first_head = lax.axis_index("head") * head_count
    base = rank * rows
    v_base = pairs * half
    valid_base = 2 * pairs * half

    barrier = pltpu.get_barrier_semaphore()
    for mask in range(1, SPAN_DEV):
        pl.semaphore_signal(barrier, inc=1, device_id={"seq": rank ^ mask}, device_id_type=MESH)
    for other in (rank + 2, rank + ranks - 2):
        pl.semaphore_signal(
            barrier, inc=1, device_id={"seq": lax.rem(other, ranks)}, device_id_type=MESH
        )

    low_lane = iota((half, PAIR), 1) < HEAD_DIM
    r_id = iota((rows, rows), 0)
    c_id = iota((rows, rows), 1)
    perm[...] = jnp.where(c_id == 2 * (r_id % half) + r_id // half, 1.0, 0.0).astype(BF16)
    unperm[...] = jnp.where(r_id == 2 * (c_id % half) + c_id // half, 1.0, 0.0).astype(BF16)
    valid_f = valid_ref[...].astype(F32)
    sorted_valid = nt(jnp.broadcast_to(valid_f, (8, rows)).astype(BF16), perm[...])[0:1]
    valid_rows[0:1] = sorted_valid[:, :half]
    valid_rows[1:2] = sorted_valid[:, half:]
    line = iota((16, 128), 0)
    lines = jnp.zeros((16, 128), F32)
    for piece in range(rows // 128):
        lines = jnp.where(line == piece, sorted_valid[:, piece * 128 : (piece + 1) * 128], lines)
    sent[pl.ds(valid_base, 16)] = lines.astype(BF16)

    def lanes_of(pair):
        return pl.ds(pl.multiple_of(pair * PAIR, PAIR), PAIR)

    def rows_of(pair, start):
        return pl.ds(pl.multiple_of(start + pair * half, half), half)

    for pair in range(pairs):
        cols = slice(pair * PAIR, (pair + 1) * PAIR)
        k_sorted = nn(perm[...], k_ref[:, cols])
        v_sorted = nn(perm[...], v_ref[:, cols])
        k_even, k_odd = k_sorted[:half], k_sorted[half:]
        v_even, v_odd = v_sorted[:half], v_sorted[half:]
        sent[pair * half : (pair + 1) * half] = jnp.where(low_lane, k_even, k_odd).astype(BF16)
        sent[v_base + pair * half : v_base + (pair + 1) * half] = jnp.where(
            low_lane, v_even, v_odd
        ).astype(BF16)
        k_other[pair] = jnp.where(low_lane, k_odd, k_even).astype(BF16)
        v_other[pair] = jnp.where(low_lane, v_odd, v_even).astype(BF16)

    pl.semaphore_wait(barrier, SPAN_DEV + 1)

    def kv_copy(mask, part):
        start = part * v_base
        size = v_base + 16 * part
        return pltpu.make_async_remote_copy(
            src_ref=sent.at[pl.ds(start, size)],
            dst_ref=got.at[mask - 1, pl.ds(start, size)],
            send_sem=kv_send.at[mask - 1, part],
            recv_sem=kv_recv.at[mask - 1, part],
            device_id={"seq": rank ^ mask},
            device_id_type=MESH,
        )

    kv_copies = {(m, part): kv_copy(m, part) for m in range(1, SPAN_DEV) for part in range(2)}
    kv_copies[2, 0].start()

    rates = rates_ref[...]
    upper = jnp.where(r_id <= c_id, 1.0, 0.0)
    lower = jnp.where(r_id >= c_id, 1.0, 0.0)
    log_all = -nn(rates, upper, HIGHEST)
    columns = -nt(lower, rates, HIGHEST)
    for head in range(head_count):
        log_col[head] = jnp.broadcast_to(columns[:, head : head + 1], (rows, 128))
    drive_all = steps_ref[...] * valid_f
    for head in range(head_count):
        log_row[head] = log_all[head : head + 1]
        drive_row[head] = drive_all[head : head + 1]
    into_t[...] = into_ref[...].astype(F32).T
    log_end = log_all[:, rows - 1 : rows]
    own_lane = iota((head_count, width), 1) // HEAD_DIM == iota((head_count, width), 0)
    own_log = jnp.sum(jnp.where(own_lane, log_end, 0.0), axis=0, keepdims=True)
    to_end = drive_all * jnp.exp(log_end - log_all)
    state_dim = into_ref.shape[1]
    low_state = iota((state_dim, PAIR), 1) < HEAD_DIM
    for pair in range(pairs):
        cols = slice(pair * PAIR, (pair + 1) * PAIR)
        parts = []
        for odd in range(2):
            head = 2 * pair + odd
            scaled = (into_t[...] * to_end[head : head + 1]).astype(BF16)
            parts.append(nn(scaled, v_ref[:, cols]))
        s_sent[0, 0:state_dim, cols] = jnp.where(low_state, parts[0], parts[1]).astype(BF16)
    tail = iota((16, width), 0)

    def tail_rows(log_sum):
        high, mid, low = three_parts(log_sum)
        return jnp.where(
            tail == 0, high, jnp.where(tail == 1, mid, jnp.where(tail == 2, low, 0.0))
        ).astype(BF16)

    s_sent[0, state_dim : state_dim + 16] = tail_rows(own_log)

    def state_copy(slot, other):
        return pltpu.make_async_remote_copy(
            src_ref=s_sent.at[slot],
            dst_ref=s_got.at[slot],
            send_sem=st_send.at[slot],
            recv_sem=st_recv.at[slot],
            device_id={"seq": other},
            device_id_type=MESH,
        )

    def summary(ref, slot):
        end = ref[slot, state_dim : state_dim + 16].astype(F32)
        return end[0:1] + end[1:2] + end[2:3], ref[slot, 0:state_dim].astype(F32)

    def joined(earlier, later):
        return earlier[0] + later[0], jnp.exp(later[0]) * earlier[1] + later[1]

    def chosen(flag, yes, no):
        return tuple(jnp.where(flag, a, b) for a, b in zip(yes, no))

    def pair_summary():
        own, partner = summary(s_sent, 0), summary(s_got, 0)
        first = rank % 2 == 0
        return joined(chosen(first, own, partner), chosen(first, partner, own))

    def put_out(item):
        s_sent[1, 0:state_dim] = item[1].astype(BF16)
        s_sent[1, state_dim : state_dim + 16] = tail_rows(item[0])

    swap = state_copy(0, rank ^ 1)
    chain = state_copy(1, lax.rem(rank + 2, ranks))
    swap.start()
    kv_copies[1, 0].start()
    kv_copies[3, 0].start()
    kv_copies[1, 1].start()

    for pair in range(pairs):
        cols = slice(pair * PAIR, (pair + 1) * PAIR)
        q_sorted = nn(perm[...], q_ref[:, cols]) * HEAD_DIM ** (-0.5)
        q_even, q_odd = q_sorted[:half], q_sorted[half:]
        q_same[pair] = jnp.where(low_lane, q_even, q_odd).astype(BF16)
        q_other[pair] = jnp.where(low_lane, q_odd, q_even).astype(BF16)
    eye = iota((half, half), 0) == iota((half, half), 1)
    for odd in range(2):
        opened[odd] = jnp.where(eye, 1.0, jnp.broadcast_to(valid_rows[odd : odd + 1], (half, half)))
    valid_cols[...] = nt(perm[...], jnp.broadcast_to(valid_f, (PAIR, rows)).astype(BF16))
    coupling[...] = jnp.where(r_id >= c_id, nt(read_ref[...], into_ref[...]), 0.0)

    def twice(column):
        return jnp.concatenate([column] * (half // 128), axis=1)

    q_line = 2 * iota((half, 128), 0)
    k_line = 2 * iota((1, half), 1)

    def plan(pair, odd):
        head = first_head + 2 * pair + odd
        group = head // group_heads
        spans = [seg_ref[group, config] for config in range(3)]
        strides = [dil_ref[group, config] for config in range(3)]
        return head, spans, strides

    def code(place, head, span, stride, missing):
        on = (place & (stride - 1)) == (head & (stride - 1))
        return jnp.where(on, place & -span, missing)

    def one(flag):
        return jnp.where(flag, 1.0, 0.0)

    def own_head(odd):
        return low_lane if odd == 0 else jnp.logical_not(low_lane)

    def local_pair(pair, _):
        same_pieces, other_pieces = [], []
        k_s = sent[rows_of(pair, 0), :]
        v_s = sent[rows_of(pair, v_base), :]
        k_o, v_o = k_other[pair], v_other[pair]
        for odd in range(2):
            head, spans, strides = plan(pair, odd)
            mine = own_head(odd)
            zero = jnp.zeros((half, PAIR), BF16)
            q_s = jnp.where(mine, q_same[pair], zero)
            q_o = jnp.where(mine, q_other[pair], zero)
            at_s = base + q_line + odd
            at_o = base + q_line + (1 - odd)
            key_s = base + k_line + odd
            key_o = base + k_line + (1 - odd)
            open_s = valid_rows[odd : odd + 1] > 0
            open_o = valid_rows[1 - odd : 2 - odd] > 0
            near_s = twice(at_s & -spans[0])
            near_o = twice(at_o & -spans[0])
            kn_s = key_s & -spans[0]
            kn_o = key_o & -spans[0]
            count = one(near_s == kn_s)
            for config in (1, 2):
                count = count + one(
                    twice(code(at_s, head, spans[config], strides[config], -1))
                    == code(key_s, head, spans[config], strides[config], -2)
                )
            count = count * opened[odd]
            a = jnp.where(count > 0, nt(q_s, k_s), NEG)
            b = jnp.where(near_s == jnp.where(open_o, kn_o, -2), nt(q_s, k_o), NEG)
            top = jnp.maximum(
                jnp.max(a, axis=1, keepdims=True), jnp.max(b, axis=1, keepdims=True)
            )
            wa = count * jnp.exp(a - top)
            wb = jnp.exp(b - top)
            total = jnp.sum(wa, axis=1, keepdims=True) + jnp.sum(wb, axis=1, keepdims=True)
            top_same[2 * pair + odd] = jnp.broadcast_to(top, (half, 128))
            total_same[2 * pair + odd] = jnp.broadcast_to(total, (half, 128))
            same_pieces.append(nn(wa.astype(BF16), v_s) + nn(wb.astype(BF16), v_o))
            a = jnp.where(near_o == jnp.where(open_s, kn_s, -2), nt(q_o, k_s), NEG)
            b = jnp.where(one(near_o == kn_o) * opened[1 - odd] > 0, nt(q_o, k_o), NEG)
            top = jnp.maximum(
                jnp.max(a, axis=1, keepdims=True), jnp.max(b, axis=1, keepdims=True)
            )
            wa = jnp.exp(a - top)
            wb = jnp.exp(b - top)
            total = jnp.sum(wa, axis=1, keepdims=True) + jnp.sum(wb, axis=1, keepdims=True)
            other_pieces.append((nn(wa.astype(BF16), v_s) + nn(wb.astype(BF16), v_o)) / total)
        acc_same[pair] = jnp.where(low_lane, same_pieces[0], same_pieces[1])
        out_other[pair] = jnp.where(low_lane, other_pieces[0], other_pieces[1])
        return 0

    def within_pair(pair, _):
        block = 128
        low_block = iota((block, PAIR), 1) < HEAD_DIM
        for step in range(rows // block):
            here = slice(step * block, (step + 1) * block)
            parts = []
            for odd in range(2):
                head = 2 * pair + odd
                at = log_col[head, here]
                tiles = []
                for back in range(step + 1):
                    there = slice(back * block, (back + 1) * block)
                    decay = jnp.exp(jnp.minimum(at - log_row[head, :, there], 0.0))
                    tiles.append(
                        (decay * coupling[here, there] * drive_row[head, :, there]).astype(BF16)
                    )
                mix = jnp.concatenate(tiles, axis=1) if step else tiles[0]
                parts.append(nn(mix, v_ref[0 : (step + 1) * block, lanes_of(pair)]))
            within[pair, here] = jnp.where(low_block, parts[0], parts[1])
        return 0

    lax.fori_loop(0, pairs // 2, within_pair, 0)
    swap.wait_recv()

    @pl.when(rank < 2)
    def _():
        put_out(pair_summary())
        chain.start()

    kv_copies[2, 1].start()
    lax.fori_loop(pairs // 2, pairs, within_pair, 0)
    lax.fori_loop(0, pairs // 2, local_pair, 0)

    @pl.when((rank >= 2) & (rank + 2 < ranks))
    def _():
        chain.wait_recv()
        put_out(joined(summary(s_got, 1), pair_summary()))
        chain.start()

    kv_copies[3, 1].start()
    lax.fori_loop(pairs // 2, pairs, local_pair, 0)

    low_rows = iota((rows, PAIR), 1) < HEAD_DIM
    same_head = jnp.where(
        iota((PAIR, PAIR), 0) // HEAD_DIM == iota((PAIR, PAIR), 1) // HEAD_DIM, 1.0, 0.0
    ).astype(BF16)

    def finish_scan(pair, _):
        cols = lanes_of(pair)
        value = v_ref[:, cols].astype(F32)
        since = jnp.exp(jnp.where(low_rows, log_col[2 * pair], log_col[2 * pair + 1]))
        carried = since * nn(read_ref[...], before_state[:, cols])
        skip = jnp.where(low_rows[0:1], skip_ref[2 * pair], skip_ref[2 * pair + 1])
        readout = within[pair] + carried + skip * value
        gate = gate_ref[:, cols].astype(F32)
        gated = readout * (gate / (1.0 + jnp.exp(-gate)))
        square = gated * gated
        high = square.astype(BF16)
        low = (square - high.astype(F32)).astype(BF16)
        mean = (nn(high, same_head) + nn(low, same_head)) * (1.0 / HEAD_DIM)
        scan_ref[:, cols] = (gated * lax.rsqrt(mean + 1e-05) * gain_ref[:, cols]).astype(BF16)
        return 0

    def far_pair(mask, last, valid_s, pair):
        pieces = []
        slot = mask - 1
        far_base = (rank ^ mask) * rows
        k_s = got[slot, rows_of(pair, 0), :]
        v_s = got[slot, rows_of(pair, v_base), :]
        scales, totals = [], []
        for odd in range(2):
            head, spans, strides = plan(pair, odd)
            q_s = jnp.where(own_head(odd), q_same[pair], jnp.zeros((half, PAIR), BF16))
            at_s = base + q_line + odd
            key_s = far_base + k_line + odd
            count = None
            for config in (1, 2):
                key_code = code(key_s, head, spans[config], strides[config], -2)
                key_code = jnp.where(valid_s[odd] > 0, key_code, -2)
                hit = one(
                    twice(code(at_s, head, spans[config], strides[config], -1)) == key_code
                )
                count = hit if count is None else count + hit
            a = jnp.where(count > 0, nt(q_s, k_s), NEG)
            old_top = top_same[2 * pair + odd]
            top = jnp.maximum(old_top, jnp.max(a, axis=1, keepdims=True))
            w = count * jnp.exp(a - twice(top))
            scale = jnp.exp(old_top - top)
            total = total_same[2 * pair + odd] * scale + jnp.sum(w, axis=1, keepdims=True)
            if not last:
                top_same[2 * pair + odd] = top
                total_same[2 * pair + odd] = total
            pieces.append(nn(w.astype(BF16), v_s))
            scales.append(scale)
            totals.append(total)
        acc = acc_same[pair] * jnp.where(low_lane, scales[0], scales[1]) + jnp.where(
            low_lane, pieces[0], pieces[1]
        )
        if not last:
            acc_same[pair] = acc
            return
        same = acc / jnp.where(low_lane, totals[0], totals[1])
        other = out_other[pair]
        even = jnp.where(low_lane, same, other) * valid_cols[0:half]
        odd_rows = jnp.where(low_lane, other, same) * valid_cols[half:]
        both = jnp.concatenate([even, odd_rows], axis=0).astype(BF16)
        att_ref[:, lanes_of(pair)] = nn(unperm[...], both).astype(BF16)

    for mask in range(1, SPAN_DEV):
        if mask == SPAN_DEV - 1:

            @pl.when((rank >= 2) & (rank + 2 >= ranks))
            def _():
                chain.wait_recv()

            has = rank >= 2
            came = summary(s_got, 1)
            came = (jnp.where(has, came[0], 0.0), jnp.where(has, came[1], 0.0))
            before = chosen(rank % 2 == 0, came, joined(came, summary(s_got, 0)))
            before_state[...] = before[1].astype(BF16)
            lax.fori_loop(0, pairs, finish_scan, 0)
        kv_copies[mask, 0].wait_recv()
        kv_copies[mask, 1].wait_recv()
        far_valid = got[mask - 1, pl.ds(valid_base, 16)].astype(F32)
        per = half // 128
        valid_s = [
            jnp.concatenate(
                [far_valid[odd * per + i : odd * per + i + 1] for i in range(per)], axis=1
            )
            for odd in range(2)
        ]

        def far(pair, _, mask=mask, valid_s=valid_s):
            far_pair(mask, mask == SPAN_DEV - 1, valid_s, pair)
            return 0

        lax.fori_loop(0, pairs, far, 0)
    for copy in kv_copies.values():
        copy.wait_send()
    swap.wait_send()

    @pl.when(rank + 2 < ranks)
    def _():
        chain.wait_send()


def per_device(
    ranks,
    query_rows,
    key_rows,
    value_rows,
    patch_valid,
    segment_lengths,
    dilation,
    step_sizes,
    decay_rates,
    state_in,
    state_out,
    gate_in,
    skip_weight,
    norm_gain,
):
    rows, width = query_rows.shape
    half = rows // 2
    pairs = width // PAIR
    heads = 2 * pairs
    state = state_in.shape[1]
    vmem = pl.BlockSpec(memory_space=pltpu.VMEM)
    smem = pl.BlockSpec(memory_space=pltpu.SMEM)
    sent_rows = 2 * pairs * half + 16
    out = jax.ShapeDtypeStruct((rows, width), BF16)
    return pl.pallas_call(
        functools.partial(kernel, ranks),
        out_shape=(out, out),
        in_specs=[smem] * 3 + [vmem] * 10,
        out_specs=(vmem, vmem),
        scratch_shapes=[
            pltpu.VMEM((rows, rows), BF16),
            pltpu.VMEM((rows, rows), BF16),
            pltpu.VMEM((pairs, half, PAIR), BF16),
            pltpu.VMEM((pairs, half, PAIR), BF16),
            pltpu.VMEM((pairs, half, PAIR), BF16),
            pltpu.VMEM((pairs, half, PAIR), BF16),
            pltpu.VMEM((sent_rows, PAIR), BF16),
            pltpu.VMEM((SPAN_DEV - 1, sent_rows, PAIR), BF16),
            pltpu.VMEM((2, half, half), F32),
            pltpu.VMEM((8, half), F32),
            pltpu.VMEM((rows, PAIR), F32),
            pltpu.VMEM((pairs, half, PAIR), F32),
            pltpu.VMEM((pairs, half, PAIR), F32),
            pltpu.VMEM((heads, half, 128), F32),
            pltpu.VMEM((heads, half, 128), F32),
            pltpu.VMEM((heads, 1, rows), F32),
            pltpu.VMEM((heads, rows, 128), F32),
            pltpu.VMEM((heads, 1, rows), F32),
            pltpu.VMEM((state, rows), F32),
            pltpu.VMEM((rows, rows), F32),
            pltpu.VMEM((pairs, rows, PAIR), F32),
            pltpu.VMEM((2, state + 16, width), BF16),
            pltpu.VMEM((2, state + 16, width), BF16),
            pltpu.VMEM((state, width), BF16),
            pltpu.SemaphoreType.DMA((SPAN_DEV - 1, 2)),
            pltpu.SemaphoreType.DMA((SPAN_DEV - 1, 2)),
            pltpu.SemaphoreType.DMA((2,)),
            pltpu.SemaphoreType.DMA((2,)),
        ],
        compiler_params=pltpu.CompilerParams(
            collective_id=0, has_side_effects=True, vmem_limit_bytes=60000 * 1024
        ),
        name="dilated_ssm",
    )(
        segment_lengths,
        dilation,
        skip_weight,
        query_rows,
        key_rows,
        value_rows,
        patch_valid.reshape(1, rows),
        step_sizes,
        decay_rates,
        state_in,
        state_out,
        gate_in,
        norm_gain.reshape(1, width),
    )


def solution(mesh):
    return jax.shard_map(
        functools.partial(per_device, mesh.shape["seq"]),
        mesh=mesh,
        in_specs=(
            P(("slide", "seq"), "head"),
            P(("slide", "seq"), "head"),
            P(("slide", "seq"), "head"),
            P(("slide", "seq")),
            P(),
            P(),
            P("head", ("slide", "seq")),
            P("head", ("slide", "seq")),
            P(("slide", "seq"), None),
            P(("slide", "seq"), None),
            P(("slide", "seq"), "head"),
            P("head"),
            P("head"),
        ),
        out_specs=(P(("slide", "seq"), "head"), P(("slide", "seq"), "head")),
        check_vma=False,
    )
```
